32 devices in a mesh: fsdp: 32 (over z, y, x, core).
Axes of the slice: x: 2, y: 2, z: 4, core: 2. Of those that a mesh axis runs over, the one named last changes fastest.
Arguments:
- block_input: float32 [32, 256, 384], P('fsdp'), may hold values from -6 to 6
- conditioning: float32 [32, 384], P('fsdp'), may hold values from -6 to 6
- cotangent: float32 [32, 256, 384], P('fsdp'), may hold values from -6 to 6
- image_counts: int32 [32], P('fsdp'), may hold values from 0 to 1, as said below
- first_params: bfloat16 [888832], P('fsdp'), may hold values from -1.5 to 1.5, as said below
- second_params: bfloat16 [1773568], P('fsdp'), may hold values from -1.5 to 1.5, as said below
Outputs:
- block_output: float32 [32, 256, 384], P('fsdp')
- input_grad: float32 [32, 256, 384], P('fsdp')
- cond_grad: float32 [32, 384], P('fsdp')
- first_grad: float32 [888832], P('fsdp')
- second_grad: float32 [1773568], P('fsdp')
The draws below stay inside these ranges and needn't reach their ends.
Inputs may be any that keep to these rules, and one draw needn't show every extreme that they name: Device j of fsdp holds image slots j * 1 to (j + 1) - 1 and uses the first image_counts[j] of them; in every draw some device uses all 1. `first_params`: entries past the first 887040 are padding. `second_params`: entries past the first 1772544 are padding.
All inputs are finite; a program needn't handle non-finite values.
Results may differ from the reference program's by a relative error of at most 0.014.
The reference program's roundings to bfloat16 on the way count: a program that leaves them out, or rounds other values in their place, can miss the bound.
Values may be sent and summed in bfloat16 or wider, within the bound.
No kernel may reach another device: no remote copies, remote signals or barrier semaphores. Data moves between devices by JAX's collectives and lax.ppermute only.
A program may use at most 128 MiB of HBM per device.

```python
import math
import jax
import jax.numpy as jnp
from jax import lax

D = 384
HEADS = 6
HEAD_DIM = 64
MLP = 1536
SEQ = 256
IMG_DEV = 1
IMAGES = 32
FIRST = 887040
FIRST_PAD = 888832
SECOND = 1772544
SECOND_PAD = 1773568
N_FSDP = 32


def segment_scale(position, bounds, scales):
    result = jnp.full(position.shape, scales[-1], jnp.float32)
    for upper_bound, factor in reversed(list(zip(bounds, scales[:-1]))):
        result = jnp.where(position < upper_bound, jnp.float32(factor), result)
    return result


def draw_image_counts(key, part):
    counts = jax.random.randint(key, (N_FSDP,), 0, IMG_DEV + 1, dtype=jnp.int32)
    position = jax.random.randint(jax.random.fold_in(key, 7), (), 0, N_FSDP, dtype=jnp.int32)
    return counts.at[position].set(IMG_DEV)


def draw_first_params(key, part):
    position = jnp.arange(FIRST_PAD, dtype=jnp.int32)
    normal_part = jax.random.truncated_normal(key, -3.0, 3.0, (FIRST_PAD,), jnp.float32)
    root_width = 1.0 / math.sqrt(D)
    bounds = [6 * D * D, FIRST]
    scales = [0.5 * root_width, 0.5, 0.5]
    return (normal_part * segment_scale(position, bounds, scales)).astype(jnp.bfloat16)


def draw_second_params(key, part):
    position = jnp.arange(SECOND_PAD, dtype=jnp.int32)
    normal_part = jax.random.truncated_normal(key, -3.0, 3.0, (SECOND_PAD,), jnp.float32)
    root_width = 1.0 / math.sqrt(D)
    qkv_end = 3 * D * D
    bias_end = qkv_end + 2 * D
    proj_end = bias_end + D * D
    pbias_end = proj_end + D
    fc1_end = pbias_end + D * MLP
    b1_end = fc1_end + MLP
    fc2_end = b1_end + MLP * D
    bounds = [qkv_end, bias_end, proj_end, pbias_end, fc1_end, b1_end, fc2_end, SECOND]
    scales = [root_width, 0.5, 3.0 * root_width, 0.5, root_width, 0.5, 1.0 / math.sqrt(MLP), 0.5, 0.5]
    factor = segment_scale(position, bounds, scales)
    column = position % (3 * D)
    in_pair = (position < qkv_end) & (column < 2 * D)
    pair_factor = root_width
    factor = jnp.where(in_pair, jnp.float32(pair_factor), factor)
    return (normal_part * factor).astype(jnp.bfloat16)


def block_levels(key, shape, cuts, smallest, top_value):
    gain, own = 1.0, jax.random.fold_in(key, 6)
    for axis_at, shards_of in cuts:
        draws = jnp.exp(jax.random.uniform(jax.random.fold_in(own, axis_at), (shards_of,), jnp.float32, smallest / len(cuts), top_value / len(cuts)))
        gain = gain * jnp.repeat(draws, shape[axis_at] // shards_of).reshape([-1 if axis == axis_at else 1 for axis in range(len(shape))])
    return gain


def centred(own_key, extent, deviation, reach, cuts=(), held_as=jnp.bfloat16):
    values = deviation * jax.random.normal(own_key, extent, jnp.float32)
    if cuts:
        values = values * block_levels(own_key, extent, cuts, -0.22, 0.18)
    return jnp.clip(values, -reach, reach).astype(held_as)


def setup_inputs(seed: int = 0) -> dict:
    keys = jax.random.split(jax.random.key(seed), 7)
    return {
        "block_input": centred(keys[0], (IMAGES, SEQ, D), 1.0, 6.0, ((0, 32),), jnp.float32),
        "conditioning": centred(keys[1], (IMAGES, D), 1.0, 6.0, ((0, 32),), jnp.float32),
        "cotangent": centred(keys[2], (IMAGES, SEQ, D), 1.0, 6.0, ((0, 32),), jnp.float32),
        "image_counts": draw_image_counts(jax.random.fold_in(keys[6], 71), 0),
        "first_params": draw_first_params(jax.random.fold_in(keys[6], 71), 0),
        "second_params": draw_second_params(jax.random.fold_in(keys[6], 71), 0),
    }


EPS = 1e-06
GELU_K = 0.7978845608028654
GELU_C = 0.044715

def contract(pattern, left_side, right_side):
    return jnp.einsum(pattern, left_side.astype(jnp.float32), right_side.astype(jnp.float32))

def outer_sum(left_side, right_side):
    return lax.dot_general(left_side, right_side, (((0,), (0,)), ((), ())), preferred_element_type=jnp.float32)

def back_product(left_side, right_side):
    return lax.dot_general(left_side, right_side, (((1,), (1,)), ((), ())), preferred_element_type=jnp.float32)

def unpack(flat_vector, layouts):
    pieces = []
    offset = 0
    for layout in layouts:
        entries = math.prod(layout)
        pieces.append(flat_vector[offset:offset + entries].reshape(layout))
        offset += entries
    return pieces

def first_layouts(features):
    return [(features, 6 * features), (6 * features,)]

def second_layouts(features, hidden_units):
    return [(features, 3 * features), (2 * features,), (features, features), (features,), (features, hidden_units), (hidden_units,), (hidden_units, features), (features,)]

def layer_norm(values):
    centered = values - lax.optimization_barrier(jnp.mean(values, axis=-1, keepdims=True))
    inverse = lax.rsqrt(lax.optimization_barrier(jnp.mean(centered * centered, axis=-1, keepdims=True)) + EPS)
    return (centered * inverse, inverse)

def norm_back(upstream, normed, inverse):
    return inverse * (upstream - lax.optimization_barrier(jnp.mean(upstream, axis=-1, keepdims=True)) - normed * lax.optimization_barrier(jnp.mean(upstream * normed, axis=-1, keepdims=True)))

def gelu_pair(hidden):
    inner_arg = GELU_K * (hidden + GELU_C * hidden * hidden * hidden)
    tangent = jnp.tanh(inner_arg)
    gelu_value = 0.5 * hidden * (1.0 + tangent)
    gelu_slope = 0.5 * (1.0 + tangent) + 0.5 * hidden * (1.0 - tangent * tangent) * GELU_K * (1.0 + 3.0 * GELU_C * hidden * hidden)
    return (gelu_value, gelu_slope)

def forward(block_input, conditioning, ada_list, block_list):
    w_ada, b_ada = ada_list
    w_qkv, b_qv, w_proj, b_proj, w_fc1, b_fc1, w_fc2, b_fc2 = block_list
    images, tokens, features = block_input.shape
    token_rows = images * tokens
    cond_sigmoid = jax.nn.sigmoid(conditioning)
    cond_act = (conditioning * cond_sigmoid).astype(jnp.bfloat16)
    modulation = jnp.dot(cond_act, w_ada, preferred_element_type=jnp.float32) + b_ada.astype(jnp.float32)
    modulators = jnp.split(modulation[:, None, :], 6, axis=2)
    shift_attn, scale_attn, gate_attn, shift_mlp, scale_mlp, gate_mlp = modulators
    normed_one, inverse_one = layer_norm(block_input)
    moved_one = (normed_one * (1.0 + scale_attn) + shift_attn).astype(jnp.bfloat16).reshape(token_rows, features)
    projected = jnp.dot(moved_one, w_qkv, preferred_element_type=jnp.float32)
    bias_wide = b_qv.astype(jnp.float32)
    head_layout = (images, tokens, HEADS, HEAD_DIM)
    query_heads = (projected[:, :features] + bias_wide[:features]).astype(jnp.bfloat16).reshape(head_layout)
    key_heads = projected[:, features:2 * features].astype(jnp.bfloat16).reshape(head_layout)
    value_heads = (projected[:, 2 * features:] + bias_wide[features:]).astype(jnp.bfloat16).reshape(head_layout)
    scores = contract('bqhd,bkhd->bhqk', query_heads, key_heads) * (1.0 / math.sqrt(HEAD_DIM))
    highest = lax.optimization_barrier(jnp.max(scores, axis=3, keepdims=True))
    totals = lax.optimization_barrier(jnp.sum(jnp.exp(scores - highest), axis=3, keepdims=True))
    log_total = highest + jnp.log(totals)
    weights = jnp.exp(scores - log_total).astype(jnp.bfloat16)
    attn_mixed = contract('bhqk,bkhd->bqhd', weights, value_heads).astype(jnp.bfloat16).reshape(token_rows, features)
    attn_out = (jnp.dot(attn_mixed, w_proj, preferred_element_type=jnp.float32) + b_proj.astype(jnp.float32)).reshape(images, tokens, features)
    after_attn = block_input + gate_attn * attn_out
    normed_two, inverse_two = layer_norm(after_attn)
    moved_two = (normed_two * (1.0 + scale_mlp) + shift_mlp).astype(jnp.bfloat16).reshape(token_rows, features)
    hidden_pre = jnp.dot(moved_two, w_fc1, preferred_element_type=jnp.float32) + b_fc1.astype(jnp.float32)
    activated, gelu_slope = gelu_pair(hidden_pre)
    activated = activated.astype(jnp.bfloat16)
    mlp_out = (jnp.dot(activated, w_fc2, preferred_element_type=jnp.float32) + b_fc2.astype(jnp.float32)).reshape(images, tokens, features)
    output = after_attn + gate_mlp * mlp_out
    return dict(output=output, conditioning=conditioning, cond_sigmoid=cond_sigmoid, cond_act=cond_act, modulators=modulators, normed_one=normed_one, inverse_one=inverse_one, moved_one=moved_one, query_heads=query_heads, key_heads=key_heads, value_heads=value_heads, log_total=log_total, attn_mixed=attn_mixed, attn_out=attn_out, normed_two=normed_two, inverse_two=inverse_two, moved_two=moved_two, gelu_slope=gelu_slope, activated=activated, mlp_out=mlp_out)

def back_mlp(cotangent, kept_state, block_list):
    w_fc1, b_fc1, w_fc2, b_fc2 = block_list[4:]
    images, tokens, features = cotangent.shape
    token_rows = images * tokens
    shift_attn, scale_attn, gate_attn, shift_mlp, scale_mlp, gate_mlp = kept_state['modulators']
    gate_grad_mlp = lax.optimization_barrier(jnp.sum(cotangent * kept_state['mlp_out'], axis=1))
    out_grad = (cotangent * gate_mlp).reshape(token_rows, features)
    out_grad_low = out_grad.astype(jnp.bfloat16)
    grad_fc2 = outer_sum(kept_state['activated'], out_grad_low)
    grad_bias2 = lax.optimization_barrier(jnp.sum(out_grad, axis=0))
    pre_grad = back_product(out_grad_low, w_fc2) * kept_state['gelu_slope']
    pre_grad_low = pre_grad.astype(jnp.bfloat16)
    grad_fc1 = outer_sum(kept_state['moved_two'], pre_grad_low)
    grad_bias1 = lax.optimization_barrier(jnp.sum(pre_grad, axis=0))
    moved_grad = back_product(pre_grad_low, w_fc1).reshape(images, tokens, features)
    shift_grad_mlp = lax.optimization_barrier(jnp.sum(moved_grad, axis=1))
    scale_grad_mlp = lax.optimization_barrier(jnp.sum(moved_grad * kept_state['normed_two'], axis=1))
    grad_after = cotangent + norm_back(moved_grad * (1.0 + scale_mlp), kept_state['normed_two'], kept_state['inverse_two'])
    mlp_flat = jnp.concatenate([grad_fc1.reshape(-1), grad_bias1, grad_fc2.reshape(-1), grad_bias2])
    return (grad_after, mlp_flat, (shift_grad_mlp, scale_grad_mlp, gate_grad_mlp))

def back_attn(grad_after, kept_state, block_list, mlp_mod):
    w_qkv, b_qv, w_proj, b_proj = block_list[:4]
    images, tokens, features = grad_after.shape
    token_rows = images * tokens
    head_layout = (images, tokens, HEADS, HEAD_DIM)
    shift_attn, scale_attn, gate_attn, shift_mlp, scale_mlp, gate_mlp = kept_state['modulators']
    gate_grad_attn = lax.optimization_barrier(jnp.sum(grad_after * kept_state['attn_out'], axis=1))
    proj_grad = (grad_after * gate_attn).reshape(token_rows, features)
    proj_grad_low = proj_grad.astype(jnp.bfloat16)
    grad_proj = outer_sum(kept_state['attn_mixed'], proj_grad_low)
    grad_bproj = lax.optimization_barrier(jnp.sum(proj_grad, axis=0))
    mixed_grad = back_product(proj_grad_low, w_proj).astype(jnp.bfloat16).reshape(head_layout)
    query_heads = kept_state['query_heads']
    key_heads = kept_state['key_heads']
    scale_factor = 1.0 / math.sqrt(HEAD_DIM)
    scores = contract('bqhd,bkhd->bhqk', query_heads, key_heads) * scale_factor
    probability = jnp.exp(scores - kept_state['log_total'])
    weights = probability.astype(jnp.bfloat16)
    value_grad = contract('bhqk,bqhd->bkhd', weights, mixed_grad)
    prob_grad = contract('bqhd,bkhd->bhqk', mixed_grad, kept_state['value_heads'])
    mixed_heads = kept_state['attn_mixed'].reshape(head_layout)
    row_dot = lax.optimization_barrier(jnp.sum(mixed_grad.astype(jnp.float32) * mixed_heads.astype(jnp.float32), axis=3))
    row_dot = jnp.transpose(row_dot, (0, 2, 1))[:, :, :, None]
    score_grad = (probability * (prob_grad - row_dot) * scale_factor).astype(jnp.bfloat16)
    query_grad = contract('bhqk,bkhd->bqhd', score_grad, key_heads)
    key_grad = contract('bhqk,bqhd->bkhd', score_grad, query_heads)
    qkv_grad = jnp.concatenate([query_grad.reshape(token_rows, features), key_grad.reshape(token_rows, features), value_grad.reshape(token_rows, features)], axis=1)
    qkv_grad_low = qkv_grad.astype(jnp.bfloat16)
    grad_qkv = outer_sum(kept_state['moved_one'], qkv_grad_low)
    grad_bqv = jnp.concatenate([lax.optimization_barrier(jnp.sum(qkv_grad[:, :features], axis=0)), lax.optimization_barrier(jnp.sum(qkv_grad[:, 2 * features:], axis=0))])
    moved_grad = back_product(qkv_grad_low, w_qkv).reshape(images, tokens, features)
    shift_grad_attn = lax.optimization_barrier(jnp.sum(moved_grad, axis=1))
    scale_grad_attn = lax.optimization_barrier(jnp.sum(moved_grad * kept_state['normed_one'], axis=1))
    input_grad = grad_after + norm_back(moved_grad * (1.0 + scale_attn), kept_state['normed_one'], kept_state['inverse_one'])
    shift_grad_mlp, scale_grad_mlp, gate_grad_mlp = mlp_mod
    mod_grad = jnp.concatenate([shift_grad_attn, scale_grad_attn, gate_grad_attn, shift_grad_mlp, scale_grad_mlp, gate_grad_mlp], axis=1)
    attn_flat = jnp.concatenate([grad_qkv.reshape(-1), grad_bqv, grad_proj.reshape(-1), grad_bproj])
    return (input_grad, mod_grad, attn_flat)

def back_ada(mod_grad, kept_state, ada_list):
    w_ada, b_ada = ada_list
    mod_grad_low = mod_grad.astype(jnp.bfloat16)
    grad_ada = outer_sum(kept_state['cond_act'], mod_grad_low)
    grad_bada = lax.optimization_barrier(jnp.sum(mod_grad, axis=0))
    sigmoid_c = kept_state['cond_sigmoid']
    cond_input = kept_state['conditioning']
    cond_grad = back_product(mod_grad_low, w_ada) * sigmoid_c * (1.0 + cond_input * (1.0 - sigmoid_c))
    return (cond_grad, jnp.concatenate([grad_ada.reshape(-1), grad_bada]))

def run_images(inputs, cond_rows, cotan_rows, valid_rows, ada_list, block_list):
    kept_state = forward(inputs, cond_rows, ada_list, block_list)
    output = kept_state['output'] * valid_rows[:, None, None]
    masked = cotan_rows * valid_rows[:, None, None]
    grad_after, mlp_flat, mlp_mod = back_mlp(masked, kept_state, block_list)
    input_grad, mod_grad, attn_flat = back_attn(grad_after, kept_state, block_list, mlp_mod)
    cond_grad, ada_flat = back_ada(mod_grad, kept_state, ada_list)
    return (output, input_grad, cond_grad, ada_flat, jnp.concatenate([attn_flat, mlp_flat]))

def reference(block_input, conditioning, cotangent, image_counts, first_params, second_params):
    ada_list = unpack(first_params, first_layouts(D))
    block_list = unpack(second_params, second_layouts(D, MLP))
    slot_ids = jnp.arange(IMAGES, dtype=jnp.int32)
    owner_ids = (slot_ids // IMG_DEV).astype(jnp.int32)
    valid_mask = (slot_ids % IMG_DEV < image_counts[owner_ids]).astype(jnp.float32)
    group_size = math.gcd(IMAGES, 16)
    group_count = IMAGES // group_size

    def one_group(running, group_data):
        inputs, cond_rows, cotan_rows, valid_rows = group_data
        output, input_grad, cond_grad, first_flat, second_flat = run_images(inputs, cond_rows, cotan_rows, valid_rows, ada_list, block_list)
        return ((running[0] + first_flat, running[1] + second_flat), (output, input_grad, cond_grad))
    group_data = (block_input.reshape(group_count, group_size, SEQ, D), conditioning.reshape(group_count, group_size, D), cotangent.reshape(group_count, group_size, SEQ, D), valid_mask.reshape(group_count, group_size))
    start = (jnp.zeros((FIRST,), jnp.float32), jnp.zeros((SECOND,), jnp.float32))
    totals, stacked = lax.scan(one_group, start, group_data)
    block_output = stacked[0].reshape(IMAGES, SEQ, D)
    input_grad = stacked[1].reshape(IMAGES, SEQ, D)
    cond_grad = stacked[2].reshape(IMAGES, D)
    first_grad = jnp.concatenate([totals[0], jnp.zeros((FIRST_PAD - FIRST,), jnp.float32)])
    second_grad = jnp.concatenate([totals[1], jnp.zeros((SECOND_PAD - SECOND,), jnp.float32)])
    return (block_output, input_grad, cond_grad, first_grad, second_grad)
```

```python
import functools
import math

import jax
import jax.numpy as jnp
from jax import lax
from jax.experimental import pallas as pl
from jax.experimental.pallas import tpu as pltpu
from jax.sharding import PartitionSpec as P

HEADS = 6
HEAD_DIM = 64
MLP = 1536
LANES = 128
CHUNK = 256

EPS = 1e-06
GELU_K = 0.7978845608028654
GELU_C = 0.044715


F32 = jnp.float32
BF16 = jnp.bfloat16


def axis_bits(mesh):
    devices = list(mesh.devices.flat)
    count = len(devices)

    def place(device):
        coords = getattr(device, "coords", None)
        if coords is None:
            return None
        return (*coords, getattr(device, "core_on_chip", 0))

    groups = {}
    bit = 1
    while bit < count:
        start, end = place(devices[0]), place(devices[bit])
        if start is None:
            key = 3 if bit == 1 else bit + 100
        else:
            key = next(axis for axis in range(4) if start[axis] != end[axis])
        groups.setdefault(key, []).append(bit)
        bit *= 2
    core = groups.pop(3, [])
    links = sorted(groups.values(), key=lambda bits: (-len(bits), bits))
    return core, links


def orders_of(links):
    return [links, links[:1] + links[1:][::-1], links[1:] + links[:1]]


def masks_of(bits):
    masks = [0]
    for bit in bits:
        masks = masks + [mask | bit for mask in masks]
    return masks


def swap(values, mask, count):
    return lax.ppermute(values, "fsdp", [(index, index ^ mask) for index in range(count)])


def gather_stage(buffer, bits, count):
    pieces = [buffer] + [swap(buffer, mask, count) for mask in masks_of(bits)[1:]]
    return jnp.concatenate(pieces, axis=0)


def reduce_stage(buffer, bits, count):
    masks = masks_of(bits)
    pieces = buffer.reshape(len(masks), buffer.shape[0] // len(masks), *buffer.shape[1:])
    moved = [swap(pieces[index], mask, count) for index, mask in enumerate(masks) if mask]
    total = pieces[0]
    for piece in moved:
        total = total + piece
    return total


def split_rows(tiles):
    last = max(1, round(0.22 * tiles))
    first = (tiles - last + 1) // 2
    return [first, tiles - last - first, last]


def up_to(value, multiple):
    return -(-value // multiple) * multiple


def dot_nn(left, right):
    return lax.dot_general(left, right, (((1,), (0,)), ((), ())), preferred_element_type=F32)


def dot_nt(left, right):
    return lax.dot_general(left, right, (((1,), (1,)), ((), ())), preferred_element_type=F32)


def dot_tn(left, right):
    return lax.dot_general(left, right, (((0,), (0,)), ((), ())), preferred_element_type=F32)


def slot_owner(device, slot, bits):
    offset = 0
    for position, bit in enumerate(bits):
        offset = offset + ((slot >> position) & 1) * bit
    return device ^ offset


def layer_norm(values):
    centered = values - jnp.mean(values, axis=-1, keepdims=True)
    inverse = lax.rsqrt(jnp.mean(centered * centered, axis=-1, keepdims=True) + EPS)
    return centered * inverse, inverse


def norm_back(upstream, normed, inverse):
    return inverse * (
        upstream
        - jnp.mean(upstream, axis=-1, keepdims=True)
        - normed * jnp.mean(upstream * normed, axis=-1, keepdims=True)
    )


def block_kernel(
    plan,
    info,
    x_ref,
    cond_ref,
    cot_ref,
    *refs,
):
    (n_in, gather_parts, rows_first, rows_second, pad_second, out_parts, D) = plan
    part_refs = refs[:n_in]
    out_ref, xgrad_ref, cgrad_ref, mod_out_ref = refs[n_in : n_in + 4]
    g_refs = refs[n_in + 4 : n_in + 4 + len(out_parts)]
    (
        flat1,
        flat2,
        wada,
        wqkv,
        wproj,
        wf1,
        wf2,
        mod_ref,
        qkv,
        prob,
        mixed,
        act,
        slope,
        dqkv,
    ) = refs[n_in + 4 + len(out_parts) :]
    device = info[0]
    valid = jnp.where(info[1] > 0, 1.0, 0.0).astype(F32)
    fr = D // LANES
    n_chunks = MLP // CHUNK
    cr = CHUNK // LANES
    mr = MLP // LANES

    for ref, (bits, core_mask, segments) in zip(part_refs, gather_parts):

        def body(slot, carry, ref=ref, bits=bits, core_mask=core_mask, segments=segments):
            owner = slot_owner(device, slot, bits) ^ core_mask
            for start, size, second, target in segments:
                piece = ref[slot, start : start + size, :].astype(F32)
                if second:
                    flat2[pl.ds(owner * rows_second + target, size), :] = piece
                else:
                    flat1[pl.ds(owner * rows_first + target, size), :] = piece
            return carry

        lax.fori_loop(0, ref.shape[0], body, 0)

    cond = cond_ref[...]
    cond_sigmoid = jax.nn.sigmoid(cond)
    cond_act = cond * cond_sigmoid
    cond_low = jnp.broadcast_to(cond_act.astype(BF16), (16, D))
    for j in range(6 * fr):
        w = flat1[pl.ds(j, D, stride=6 * fr), :].astype(BF16)
        wada[j] = w
        bias = flat1[pl.ds(6 * fr * D + j, 1), :]
        mod_ref[0:1, j * LANES : (j + 1) * LANES] = dot_nn(cond_low, w)[0:1] + bias

    def mod_piece(index):
        return mod_ref[0:1, index * D : (index + 1) * D]

    o_bqv = 3 * fr * D
    o_proj = o_bqv + 2 * fr
    o_bproj = o_proj + fr * D
    o_fc1 = o_bproj + fr
    o_b1 = o_fc1 + mr * D
    o_fc2 = o_b1 + mr
    o_b2 = o_fc2 + fr * MLP
    o_end = o_b2 + fr
    for j in range(3 * fr):
        wqkv[:, j * LANES : (j + 1) * LANES] = flat2[pl.ds(j, D, stride=3 * fr), :].astype(BF16)
    for j in range(fr):
        wproj[:, j * LANES : (j + 1) * LANES] = flat2[pl.ds(o_proj + j, D, stride=fr), :].astype(
            BF16
        )
    for c in range(n_chunks):
        for j in range(cr):
            wf1[c, :, j * LANES : (j + 1) * LANES] = flat2[
                pl.ds(o_fc1 + c * cr + j, D, stride=mr), :
            ].astype(BF16)
        for j in range(fr):
            wf2[c, :, j * LANES : (j + 1) * LANES] = flat2[
                pl.ds(o_fc2 + c * CHUNK * fr + j, CHUNK, stride=fr), :
            ].astype(BF16)

    def bias_row(start, rows):
        return jnp.concatenate([flat2[pl.ds(start + i, 1), :] for i in range(rows)], axis=1)

    block_input = x_ref[...]
    normed_one, inverse_one = layer_norm(block_input)
    moved_one = (normed_one * (1.0 + mod_piece(1)) + mod_piece(0)).astype(BF16)
    projected = dot_nn(moved_one, wqkv[...])
    bias_qv = bias_row(o_bqv, 2 * fr)
    for j in range(fr):
        cols = slice(j * LANES, (j + 1) * LANES)
        qkv[j] = (projected[:, cols] + bias_qv[:, cols]).astype(BF16)
        qkv[fr + j] = projected[:, D + j * LANES : D + (j + 1) * LANES].astype(BF16)
        qkv[2 * fr + j] = (
            projected[:, 2 * D + j * LANES : 2 * D + (j + 1) * LANES]
            + bias_qv[:, D + j * LANES : D + (j + 1) * LANES]
        ).astype(BF16)
    scale_factor = 1.0 / math.sqrt(HEAD_DIM)
    low_lane = lax.broadcasted_iota(jnp.int32, (1, LANES), 1) < HEAD_DIM
    lane_masks = [
        jnp.where(low_lane, 1.0, 0.0).astype(BF16),
        jnp.where(low_lane, 0.0, 1.0).astype(BF16),
    ]
    for p in range(fr):
        q, k, v = qkv[p], qkv[fr + p], qkv[2 * fr + p]
        outs = []
        for h in range(2):
            scores = dot_nt(q * lane_masks[h], k) * scale_factor
            raised = jnp.exp(scores - jnp.max(scores, axis=1, keepdims=True))
            probability = raised * (1.0 / jnp.sum(raised, axis=1, keepdims=True))
            prob[2 * p + h] = probability
            outs.append(dot_nn(probability.astype(BF16), v))
        mixed[:, p * LANES : (p + 1) * LANES] = jnp.where(low_lane, outs[0], outs[1]).astype(BF16)
    attn_out = dot_nn(mixed[...], wproj[...]) + bias_row(o_bproj, fr)
    after_attn = block_input + mod_piece(2) * attn_out
    normed_two, inverse_two = layer_norm(after_attn)
    moved_two = (normed_two * (1.0 + mod_piece(4)) + mod_piece(3)).astype(BF16)

    mlp_out = jnp.zeros_like(after_attn) + bias_row(o_b2, fr)
    for c in range(n_chunks):
        hidden = dot_nn(moved_two, wf1[c]) + bias_row(o_b1 + c * cr, cr)
        square = hidden * hidden
        tangent = jnp.tanh(GELU_K * (hidden + GELU_C * square * hidden))
        half = 0.5 * (1.0 + tangent)
        low = (hidden * half).astype(BF16)
        act[c] = low
        slope[c] = half + 0.5 * hidden * (1.0 - tangent * tangent) * (
            GELU_K + (3.0 * GELU_C * GELU_K) * square
        )
        mlp_out = mlp_out + dot_nn(low, wf2[c])
    gate_mlp = mod_piece(5)
    out_ref[...] = valid * (after_attn + gate_mlp * mlp_out)

    masked = valid * cot_ref[...]
    gate_grad_mlp = jnp.sum(masked * mlp_out, axis=0, keepdims=True)
    out_grad = masked * gate_mlp
    out_grad_low = out_grad.astype(BF16)

    def put_row(start, row):
        for i in range(row.shape[1] // LANES):
            flat2[pl.ds(start + i, 1), :] = row[:, i * LANES : (i + 1) * LANES]

    put_row(o_b2, jnp.sum(out_grad, axis=0, keepdims=True))
    moved_grad = jnp.zeros_like(after_attn)
    for c in range(n_chunks):
        pre_grad = dot_nt(out_grad_low, wf2[c]) * slope[c]
        put_row(o_b1 + c * cr, jnp.sum(pre_grad, axis=0, keepdims=True))
        pre_low = pre_grad.astype(BF16)
        grad2 = dot_tn(act[c], out_grad_low)
        for j in range(fr):
            flat2[pl.ds(o_fc2 + c * CHUNK * fr + j, CHUNK, stride=fr), :] = grad2[
                :, j * LANES : (j + 1) * LANES
            ]
        grad1 = dot_tn(moved_two, pre_low)
        for j in range(cr):
            flat2[pl.ds(o_fc1 + c * cr + j, D, stride=mr), :] = grad1[
                :, j * LANES : (j + 1) * LANES
            ]
        moved_grad = moved_grad + dot_nt(pre_low, wf1[c])
    shift_grad_mlp = jnp.sum(moved_grad, axis=0, keepdims=True)
    scale_grad_mlp = jnp.sum(moved_grad * normed_two, axis=0, keepdims=True)
    grad_after = masked + norm_back(moved_grad * (1.0 + mod_piece(4)), normed_two, inverse_two)

    gate_grad_attn = jnp.sum(grad_after * attn_out, axis=0, keepdims=True)
    proj_grad = grad_after * mod_piece(2)
    proj_low = proj_grad.astype(BF16)
    grad_proj = dot_tn(mixed[...], proj_low)
    for j in range(fr):
        flat2[pl.ds(o_proj + j, D, stride=fr), :] = grad_proj[:, j * LANES : (j + 1) * LANES]
    put_row(o_bproj, jnp.sum(proj_grad, axis=0, keepdims=True))
    mixed_grad = dot_nt(proj_low, wproj[...]).astype(BF16)
    for p in range(fr):
        q, k, v = qkv[p], qkv[fr + p], qkv[2 * fr + p]
        cols = slice(p * LANES, (p + 1) * LANES)
        pair_grad = mixed_grad[:, cols]
        product = pair_grad.astype(F32) * mixed[:, cols].astype(F32)
        pieces = []
        for h in range(2):
            probability = prob[2 * p + h]
            value_grad = dot_tn(probability.astype(BF16), pair_grad)
            prob_grad = dot_nt(pair_grad * lane_masks[h], v)
            own = jnp.where(low_lane, product, 0.0) if h == 0 else jnp.where(low_lane, 0.0, product)
            row_dot = jnp.sum(own, axis=1, keepdims=True)
            score_grad = (probability * (prob_grad - row_dot) * scale_factor).astype(BF16)
            pieces.append((dot_nn(score_grad, k), dot_tn(score_grad, q), value_grad))
        for index in range(3):
            grad = jnp.where(low_lane, pieces[0][index], pieces[1][index])
            if index != 1:
                put_row(
                    o_bqv + (0 if index == 0 else fr) + p, jnp.sum(grad, axis=0, keepdims=True)
                )
            dqkv[:, index * D + p * LANES : index * D + (p + 1) * LANES] = grad.astype(BF16)
    grad_qkv = dot_tn(moved_one, dqkv[...])
    for j in range(3 * fr):
        flat2[pl.ds(j, D, stride=3 * fr), :] = grad_qkv[:, j * LANES : (j + 1) * LANES]
    moved_grad_one = dot_nt(dqkv[...], wqkv[...])
    shift_grad_attn = jnp.sum(moved_grad_one, axis=0, keepdims=True)
    scale_grad_attn = jnp.sum(moved_grad_one * normed_one, axis=0, keepdims=True)
    xgrad_ref[...] = grad_after + norm_back(
        moved_grad_one * (1.0 + mod_piece(1)), normed_one, inverse_one
    )

    mod_rows = [
        shift_grad_attn,
        scale_grad_attn,
        gate_grad_attn,
        shift_grad_mlp,
        scale_grad_mlp,
        gate_grad_mlp,
    ]
    cond_back = jnp.zeros((16, D), F32)
    mod_out_ref[...] = jnp.zeros_like(mod_out_ref)
    for index, row in enumerate(mod_rows):
        for i in range(fr):
            j = index * fr + i
            piece = row[:, i * LANES : (i + 1) * LANES]
            mod_out_ref[j : j + 1, :] = piece
            low = jnp.broadcast_to(piece.astype(BF16), (16, LANES))
            cond_back = cond_back + dot_nt(low, wada[j])
    for i in range(fr):
        j = 6 * fr + i
        mod_out_ref[j : j + 1, :] = cond_act.astype(BF16).astype(F32)[
            :, i * LANES : (i + 1) * LANES
        ]
    cgrad_ref[...] = cond_back[0:1] * cond_sigmoid * (1.0 + cond * (1.0 - cond_sigmoid))

    flat2[o_end : flat2.shape[0], :] = jnp.zeros((flat2.shape[0] - o_end, LANES), F32)
    for ref, (bits, start, rows) in zip(g_refs, out_parts):

        def body(slot, carry, ref=ref, bits=bits, start=start, rows=rows):
            owner = slot_owner(device, slot, bits)
            ref[slot] = flat2[pl.ds(owner * rows_second + start, rows), :]
            return carry

        lax.fori_loop(0, ref.shape[0], body, 0)


def ada_kernel(rows_first, D, info, gathered_ref, out_ref, flat):
    device = info[0]
    fr = D // LANES
    wide = 6 * fr
    images = gathered_ref.shape[0]
    first = (device * rows_first) // wide
    shift = device * rows_first - first * wide
    take = flat.shape[0] // wide
    picked = jnp.zeros((images, take), F32)
    for i in range(fr):
        rows = lax.broadcasted_iota(jnp.int32, (LANES, take), 0) + i * LANES
        chosen = lax.broadcasted_iota(jnp.int32, (LANES, take), 1) + first
        onehot = jnp.where(rows == chosen, 1.0, 0.0).astype(BF16)
        picked = picked + dot_nn(gathered_ref[:, wide + i, :].astype(BF16), onehot)
    picked = picked.astype(BF16)
    row_ids = lax.broadcasted_iota(jnp.int32, (take, LANES), 0) + first
    for j in range(wide):
        grads = gathered_ref[:, j, :]
        product = dot_tn(picked, grads.astype(BF16))
        total = jnp.sum(grads, axis=0, keepdims=True)
        flat[pl.ds(j, take, stride=wide), :] = jnp.where(row_ids == D, total, product)
    out_ref[...] = flat[pl.ds(shift, rows_first), :]


def vmem():
    return pl.BlockSpec(memory_space=pltpu.VMEM)


def on_device(mesh, block_input, conditioning, cotangent, image_counts, first_params, second_params):
    count = mesh.shape["fsdp"]
    images, tokens, D = block_input.shape
    core, links = axis_bits(mesh)
    orders = orders_of(links)
    device = lax.axis_index("fsdp").astype(jnp.int32)
    info = jnp.stack([device, image_counts[0]])
    rows_first = first_params.shape[0] // LANES
    rows_second = second_params.shape[0] // LANES
    pad_first, pad_second = up_to(rows_first, 16), up_to(rows_second, 16)

    def rows_of(vector, rows, padded):
        return jnp.pad(vector.reshape(rows, LANES), ((0, padded - rows), (0, 0)))

    shard = jnp.concatenate(
        [
            rows_of(second_params, rows_second, pad_second),
            rows_of(first_params, rows_first, pad_first),
        ]
    )
    bounds = [0]
    for tiles in split_rows(shard.shape[0] // 16):
        bounds.append(bounds[-1] + 16 * tiles)
    buffers = [shard[None, bounds[i] : bounds[i + 1]] for i in range(3)]
    for stage in range(len(links)):
        buffers = [gather_stage(buffers[i], orders[i][stage], count) for i in range(3)]
    gathered, gather_parts = [], []
    for i in range(3):
        start, end = bounds[i], bounds[i + 1]
        segments = []
        low, high = start, min(end, rows_second)
        if low < high:
            segments.append((0, high - low, True, low))
        low, high = max(start, pad_second), min(end, pad_second + rows_first)
        if low < high:
            segments.append((low - start, high - low, False, low - pad_second))
        bits = tuple(bit for group in orders[i] for bit in group)
        for mask in masks_of(core):
            gathered.append(swap(buffers[i], mask, count) if mask else buffers[i])
            gather_parts.append((bits, mask, tuple(segments)))

    pad_out = up_to(rows_second, 8)
    out_parts = []
    start = 0
    for i, tiles in enumerate(split_rows(pad_out // 8)):
        bits = tuple(bit for group in orders[i] for bit in group) + tuple(core)
        out_parts.append((bits, start, 8 * tiles))
        start += 8 * tiles
    n_chunks = MLP // CHUNK
    plan = (
        len(gathered),
        gather_parts,
        rows_first,
        rows_second,
        pad_second,
        out_parts,
        D,
    )
    sds = jax.ShapeDtypeStruct
    results = pl.pallas_call(
        functools.partial(block_kernel, plan),
        out_shape=[
            sds((tokens, D), F32),
            sds((tokens, D), F32),
            sds((1, D), F32),
            sds((up_to(7 * D // LANES, 8), LANES), F32),
        ]
        + [sds((count, rows, LANES), F32) for _, _, rows in out_parts],
        in_specs=[pl.BlockSpec(memory_space=pltpu.SMEM)] + [vmem()] * (3 + len(gathered)),
        out_specs=[vmem()] * (4 + len(out_parts)),
        scratch_shapes=[
            pltpu.VMEM((count * rows_first, LANES), F32),
            pltpu.VMEM((count * rows_second + 16, LANES), F32),
            pltpu.VMEM((6 * D // LANES, D, LANES), BF16),
            pltpu.VMEM((D, 3 * D), BF16),
            pltpu.VMEM((D, D), BF16),
            pltpu.VMEM((n_chunks, D, CHUNK), BF16),
            pltpu.VMEM((n_chunks, CHUNK, D), BF16),
            pltpu.VMEM((8, 6 * D), F32),
            pltpu.VMEM((3 * D // LANES, tokens, LANES), BF16),
            pltpu.VMEM((HEADS, tokens, tokens), F32),
            pltpu.VMEM((tokens, D), BF16),
            pltpu.VMEM((n_chunks, tokens, CHUNK), BF16),
            pltpu.VMEM((n_chunks, tokens, CHUNK), F32),
            pltpu.VMEM((tokens, 3 * D), BF16),
        ],
        compiler_params=pltpu.CompilerParams(vmem_limit_bytes=60 * 1024 * 1024),
        cost_estimate=pl.CostEstimate(
            flops=3 * 2 * tokens * D * 12 * D, bytes_accessed=16 << 20, transcendentals=1 << 20
        ),
        name="block",
    )(
        info,
        block_input.reshape(tokens, D),
        conditioning,
        cotangent.reshape(tokens, D),
        *gathered,
    )
    block_output, input_grad, cond_grad, mod_rows = results[:4]

    buffers = list(results[4:])
    every = mod_rows[None]
    for bits in core:
        buffers = [reduce_stage(buffer, [bits], count) for buffer in buffers]
    for stage in reversed(range(len(links))):
        buffers = [reduce_stage(buffers[i], orders[i][stage], count) for i in range(3)]
    for bits in links + ([core] if core else []):
        every = gather_stage(every, bits, count)
    second_grad = jnp.concatenate([buffer[0] for buffer in buffers])[:rows_second].reshape(-1)

    take = up_to((rows_first + 6 * D // LANES - 1) // (6 * D // LANES) + 1, 8)
    first_grad = pl.pallas_call(
        functools.partial(ada_kernel, rows_first, D),
        out_shape=sds((rows_first, LANES), F32),
        in_specs=[pl.BlockSpec(memory_space=pltpu.SMEM), vmem()],
        out_specs=vmem(),
        scratch_shapes=[pltpu.VMEM((take * 6 * D // LANES, LANES), F32)],
        name="ada",
    )(info, every).reshape(-1)
    return (
        block_output.reshape(block_input.shape),
        input_grad.reshape(block_input.shape),
        cond_grad,
        first_grad,
        second_grad,
    )


def solution(mesh):
    return jax.shard_map(
        functools.partial(on_device, mesh),
        mesh=mesh,
        in_specs=(
            P("fsdp", None, None),
            P("fsdp", None),
            P("fsdp", None, None),
            P("fsdp"),
            P("fsdp"),
            P("fsdp"),
        ),
        out_specs=(
            P("fsdp", None, None),
            P("fsdp", None, None),
            P("fsdp", None),
            P("fsdp"),
            P("fsdp"),
        ),
        check_vma=False,
    )
```

```python
import functools
import math

import jax
import jax.numpy as jnp
from jax import lax
from jax.experimental import pallas as pl
from jax.experimental.pallas import tpu as pltpu
from jax.sharding import PartitionSpec as P

HEADS = 6
HEAD_DIM = 64
MLP = 1536
LANES = 128
CHUNK = 256

EPS = 1e-06
GELU_K = 0.7978845608028654
GELU_C = 0.044715


F32 = jnp.float32
BF16 = jnp.bfloat16


def axis_bits(mesh):
    devices = list(mesh.devices.flat)
    count = len(devices)

    def place(device):
        coords = getattr(device, "coords", None)
        if coords is None:
            return None
        return (*coords, getattr(device, "core_on_chip", 0))

    groups = {}
    bit = 1
    while bit < count:
        start, end = place(devices[0]), place(devices[bit])
        if start is None:
            key = 3 if bit == 1 else bit + 100
        else:
            key = next(axis for axis in range(4) if start[axis] != end[axis])
        groups.setdefault(key, []).append(bit)
        bit *= 2
    core = groups.pop(3, [])
    links = sorted(groups.values(), key=lambda bits: (-len(bits), bits))
    return core, links


def stages_of(core, links):
    other = links[:1] + links[1:][::-1]
    if not core or [len(bits) for bits in other] != [len(bits) for bits in links]:
        other = links
    return list(zip(links, other))


def masks_of(bits):
    masks = [0]
    for bit in bits:
        masks = masks + [mask | bit for mask in masks]
    return masks


def pair_masks(stage):
    return list(zip(masks_of(stage[0]), masks_of(stage[1])))


def swap(values, masks, count, core):
    side = sum(core)
    pairs = [(index, index ^ masks[1 if index & side else 0]) for index in range(count)]
    return lax.ppermute(values, "fsdp", pairs)


def up_to(value, multiple):
    return -(-value // multiple) * multiple


def dot_nn(left, right):
    return lax.dot_general(left, right, (((1,), (0,)), ((), ())), preferred_element_type=F32)


def dot_nt(left, right):
    return lax.dot_general(left, right, (((1,), (1,)), ((), ())), preferred_element_type=F32)


def dot_tn(left, right):
    return lax.dot_general(left, right, (((0,), (0,)), ((), ())), preferred_element_type=F32)


def slot_owner(device, slot, bit_pair, side):
    offsets = []
    for bits in bit_pair:
        offset = 0
        for position, bit in enumerate(bits):
            offset = offset + ((slot >> position) & 1) * bit
        offsets.append(offset)
    if bit_pair[0] == bit_pair[1]:
        return device ^ offsets[0]
    return device ^ jnp.where((device & side) > 0, offsets[1], offsets[0])


TOP = 32000.0


def exponent_of(values):
    top = jnp.max(jnp.abs(values), axis=0, keepdims=True)
    return jnp.ceil(jnp.log2(jnp.maximum(top, 1e-30) * (1.0 / TOP)))


def nearest(values):
    return jnp.floor(values + 0.5)


def encode(values):
    rows = values.shape[0]
    exponent = exponent_of(values)
    coded = nearest(values * jnp.exp2(-exponent))
    last = lax.broadcasted_iota(jnp.int32, values.shape, 0) == rows - 1
    return jnp.where(last, exponent, coded).astype(jnp.int32).astype(jnp.int16)


def decode(coded):
    wide = coded.astype(jnp.int32).astype(F32)
    return wide * jnp.exp2(wide[coded.shape[0] - 1 :])


def encode_wide(values):
    exponent = exponent_of(values)
    scaled = values * jnp.exp2(-exponent)
    high = nearest(scaled)
    low = nearest((scaled - high) * TOP)
    tail = jnp.broadcast_to(exponent, (wide_rows(values.shape[0]) - 2 * values.shape[0], LANES))
    return jnp.concatenate([high, low, tail]).astype(jnp.int32).astype(jnp.int16)


def decode_wide(coded, rows):
    wide = coded.astype(jnp.int32).astype(F32)
    value = wide[:rows] + wide[rows : 2 * rows] * (1.0 / TOP)
    return value * jnp.exp2(wide[2 * rows : 2 * rows + 1])


def wide_rows(rows):
    return up_to(2 * rows + 8, 16)


def layer_norm(values):
    centered = values - jnp.mean(values, axis=-1, keepdims=True)
    inverse = lax.rsqrt(jnp.mean(centered * centered, axis=-1, keepdims=True) + EPS)
    return centered * inverse, inverse


def norm_back(upstream, normed, inverse):
    return inverse * (
        upstream
        - jnp.mean(upstream, axis=-1, keepdims=True)
        - normed * jnp.mean(upstream * normed, axis=-1, keepdims=True)
    )


def block_kernel(
    plan,
    info,
    x_ref,
    cond_ref,
    cot_ref,
    *refs,
):
    (n_in, gather_parts, rows_first, rows_second, pad_second, out_bits, out_rows, core_masks, D) = plan
    side = core_masks[-1]
    part_refs = refs[:n_in]
    out_ref, xgrad_ref, cgrad_ref, mod_out_ref, keep_ref = refs[n_in : n_in + 5]
    message_refs = refs[n_in + 5 : -15]
    (
        flat1,
        flat2,
        wada,
        wqkv,
        wproj,
        wf1,
        wf2,
        mod_ref,
        qkv,
        prob,
        mixed,
        act,
        slope,
        dqkv,
        mod_rows_ref,
    ) = refs[-15:]
    device = info[0]
    valid = jnp.where(info[1] > 0, 1.0, 0.0).astype(F32)
    fr = D // LANES
    n_chunks = MLP // CHUNK
    cr = CHUNK // LANES
    mr = MLP // LANES

    for ref, (bits, mask, core_mask, segments) in zip(part_refs, gather_parts):

        def body(
            slot, carry, ref=ref, bits=bits, mask=mask, core_mask=core_mask, segments=segments
        ):
            base = device ^ core_mask
            owner = slot_owner(base, slot, bits, side)
            if mask[0] == mask[1]:
                owner = owner ^ mask[0]
            else:
                owner = owner ^ jnp.where((base & side) > 0, mask[1], mask[0])
            for start, size, second, target in segments:
                piece = ref[slot, start : start + size, :].astype(F32)
                if second:
                    flat2[pl.ds(owner * rows_second + target, size), :] = piece
                else:
                    flat1[pl.ds(owner * rows_first + target, size), :] = piece
            return carry

        lax.fori_loop(0, ref.shape[0], body, 0)

    cond = cond_ref[...]
    cond_sigmoid = jax.nn.sigmoid(cond)
    cond_act = cond * cond_sigmoid
    cond_low = jnp.broadcast_to(cond_act.astype(BF16), (16, D))
    for j in range(6 * fr):
        w = flat1[pl.ds(j, D, stride=6 * fr), :].astype(BF16)
        wada[j] = w
        bias = flat1[pl.ds(6 * fr * D + j, 1), :]
        mod_ref[0:1, j * LANES : (j + 1) * LANES] = dot_nn(cond_low, w)[0:1] + bias

    def mod_piece(index):
        return mod_ref[0:1, index * D : (index + 1) * D]

    o_bqv = 3 * fr * D
    o_proj = o_bqv + 2 * fr
    o_bproj = o_proj + fr * D
    o_fc1 = o_bproj + fr
    o_b1 = o_fc1 + mr * D
    o_fc2 = o_b1 + mr
    o_b2 = o_fc2 + fr * MLP
    o_end = o_b2 + fr
    for j in range(3 * fr):
        wqkv[:, j * LANES : (j + 1) * LANES] = flat2[pl.ds(j, D, stride=3 * fr), :].astype(BF16)
    for j in range(fr):
        wproj[:, j * LANES : (j + 1) * LANES] = flat2[pl.ds(o_proj + j, D, stride=fr), :].astype(
            BF16
        )
    for c in range(n_chunks):
        for j in range(cr):
            wf1[c, :, j * LANES : (j + 1) * LANES] = flat2[
                pl.ds(o_fc1 + c * cr + j, D, stride=mr), :
            ].astype(BF16)
        for j in range(fr):
            wf2[c, :, j * LANES : (j + 1) * LANES] = flat2[
                pl.ds(o_fc2 + c * CHUNK * fr + j, CHUNK, stride=fr), :
            ].astype(BF16)

    def bias_row(start, rows):
        return jnp.concatenate([flat2[pl.ds(start + i, 1), :] for i in range(rows)], axis=1)

    block_input = x_ref[...]
    normed_one, inverse_one = layer_norm(block_input)
    moved_one = (normed_one * (1.0 + mod_piece(1)) + mod_piece(0)).astype(BF16)
    projected = dot_nn(moved_one, wqkv[...])
    bias_qv = bias_row(o_bqv, 2 * fr)
    for j in range(fr):
        cols = slice(j * LANES, (j + 1) * LANES)
        qkv[j] = (projected[:, cols] + bias_qv[:, cols]).astype(BF16)
        qkv[fr + j] = projected[:, D + j * LANES : D + (j + 1) * LANES].astype(BF16)
        qkv[2 * fr + j] = (
            projected[:, 2 * D + j * LANES : 2 * D + (j + 1) * LANES]
            + bias_qv[:, D + j * LANES : D + (j + 1) * LANES]
        ).astype(BF16)
    scale_factor = 1.0 / math.sqrt(HEAD_DIM)
    low_lane = lax.broadcasted_iota(jnp.int32, (1, LANES), 1) < HEAD_DIM
    lane_masks = [
        jnp.where(low_lane, 1.0, 0.0).astype(BF16),
        jnp.where(low_lane, 0.0, 1.0).astype(BF16),
    ]
    for p in range(fr):
        q, k, v = qkv[p], qkv[fr + p], qkv[2 * fr + p]
        outs = []
        for h in range(2):
            scores = dot_nt(q * lane_masks[h], k) * scale_factor
            raised = jnp.exp(scores - jnp.max(scores, axis=1, keepdims=True))
            probability = raised * (1.0 / jnp.sum(raised, axis=1, keepdims=True))
            prob[2 * p + h] = probability
            outs.append(dot_nn(probability.astype(BF16), v))
        mixed[:, p * LANES : (p + 1) * LANES] = jnp.where(low_lane, outs[0], outs[1]).astype(BF16)
    attn_out = dot_nn(mixed[...], wproj[...]) + bias_row(o_bproj, fr)
    after_attn = block_input + mod_piece(2) * attn_out
    normed_two, inverse_two = layer_norm(after_attn)
    moved_two = (normed_two * (1.0 + mod_piece(4)) + mod_piece(3)).astype(BF16)

    mlp_out = jnp.zeros_like(after_attn) + bias_row(o_b2, fr)
    for c in range(n_chunks):
        hidden = dot_nn(moved_two, wf1[c]) + bias_row(o_b1 + c * cr, cr)
        square = hidden * hidden
        tangent = jnp.tanh(GELU_K * (hidden + GELU_C * square * hidden))
        half = 0.5 * (1.0 + tangent)
        low = (hidden * half).astype(BF16)
        act[c] = low
        slope[c] = half + 0.5 * hidden * (1.0 - tangent * tangent) * (
            GELU_K + (3.0 * GELU_C * GELU_K) * square
        )
        mlp_out = mlp_out + dot_nn(low, wf2[c])
    gate_mlp = mod_piece(5)
    out_ref[...] = valid * (after_attn + gate_mlp * mlp_out)

    masked = valid * cot_ref[...]
    gate_grad_mlp = jnp.sum(masked * mlp_out, axis=0, keepdims=True)
    out_grad = masked * gate_mlp
    out_grad_low = out_grad.astype(BF16)

    def put_row(start, row):
        for i in range(row.shape[1] // LANES):
            flat2[pl.ds(start + i, 1), :] = row[:, i * LANES : (i + 1) * LANES]

    put_row(o_b2, jnp.sum(out_grad, axis=0, keepdims=True))
    moved_grad = jnp.zeros_like(after_attn)
    for c in range(n_chunks):
        pre_grad = dot_nt(out_grad_low, wf2[c]) * slope[c]
        put_row(o_b1 + c * cr, jnp.sum(pre_grad, axis=0, keepdims=True))
        pre_low = pre_grad.astype(BF16)
        grad2 = dot_tn(act[c], out_grad_low)
        for j in range(fr):
            flat2[pl.ds(o_fc2 + c * CHUNK * fr + j, CHUNK, stride=fr), :] = grad2[
                :, j * LANES : (j + 1) * LANES
            ]
        grad1 = dot_tn(moved_two, pre_low)
        for j in range(cr):
            flat2[pl.ds(o_fc1 + c * cr + j, D, stride=mr), :] = grad1[
                :, j * LANES : (j + 1) * LANES
            ]
        moved_grad = moved_grad + dot_nt(pre_low, wf1[c])
    shift_grad_mlp = jnp.sum(moved_grad, axis=0, keepdims=True)
    scale_grad_mlp = jnp.sum(moved_grad * normed_two, axis=0, keepdims=True)
    grad_after = masked + norm_back(moved_grad * (1.0 + mod_piece(4)), normed_two, inverse_two)

    gate_grad_attn = jnp.sum(grad_after * attn_out, axis=0, keepdims=True)
    proj_grad = grad_after * mod_piece(2)
    proj_low = proj_grad.astype(BF16)
    grad_proj = dot_tn(mixed[...], proj_low)
    for j in range(fr):
        flat2[pl.ds(o_proj + j, D, stride=fr), :] = grad_proj[:, j * LANES : (j + 1) * LANES]
    put_row(o_bproj, jnp.sum(proj_grad, axis=0, keepdims=True))
    mixed_grad = dot_nt(proj_low, wproj[...]).astype(BF16)
    for p in range(fr):
        q, k, v = qkv[p], qkv[fr + p], qkv[2 * fr + p]
        cols = slice(p * LANES, (p + 1) * LANES)
        pair_grad = mixed_grad[:, cols]
        product = pair_grad.astype(F32) * mixed[:, cols].astype(F32)
        pieces = []
        for h in range(2):
            probability = prob[2 * p + h]
            value_grad = dot_tn(probability.astype(BF16), pair_grad)
            prob_grad = dot_nt(pair_grad * lane_masks[h], v)
            own = jnp.where(low_lane, product, 0.0) if h == 0 else jnp.where(low_lane, 0.0, product)
            row_dot = jnp.sum(own, axis=1, keepdims=True)
            score_grad = (probability * (prob_grad - row_dot) * scale_factor).astype(BF16)
            pieces.append((dot_nn(score_grad, k), dot_tn(score_grad, q), value_grad))
        for index in range(3):
            grad = jnp.where(low_lane, pieces[0][index], pieces[1][index])
            if index != 1:
                put_row(
                    o_bqv + (0 if index == 0 else fr) + p, jnp.sum(grad, axis=0, keepdims=True)
                )
            dqkv[:, index * D + p * LANES : index * D + (p + 1) * LANES] = grad.astype(BF16)
    grad_qkv = dot_tn(moved_one, dqkv[...])
    for j in range(3 * fr):
        flat2[pl.ds(j, D, stride=3 * fr), :] = grad_qkv[:, j * LANES : (j + 1) * LANES]
    moved_grad_one = dot_nt(dqkv[...], wqkv[...])
    shift_grad_attn = jnp.sum(moved_grad_one, axis=0, keepdims=True)
    scale_grad_attn = jnp.sum(moved_grad_one * normed_one, axis=0, keepdims=True)
    xgrad_ref[...] = grad_after + norm_back(
        moved_grad_one * (1.0 + mod_piece(1)), normed_one, inverse_one
    )

    mod_rows = [
        shift_grad_attn,
        scale_grad_attn,
        gate_grad_attn,
        shift_grad_mlp,
        scale_grad_mlp,
        gate_grad_mlp,
    ]
    cond_back = jnp.zeros((16, D), F32)
    mod_rows_ref[...] = jnp.zeros_like(mod_rows_ref)
    for index, row in enumerate(mod_rows):
        for i in range(fr):
            j = index * fr + i
            piece = row[:, i * LANES : (i + 1) * LANES]
            mod_rows_ref[j : j + 1, :] = piece
            low = jnp.broadcast_to(piece.astype(BF16), (16, LANES))
            cond_back = cond_back + dot_nt(low, wada[j])
    for i in range(fr):
        j = 6 * fr + i
        mod_rows_ref[j : j + 1, :] = cond_act.astype(BF16).astype(F32)[
            :, i * LANES : (i + 1) * LANES
        ]
    mod_coded = encode_wide(mod_rows_ref[...])
    mod_out_ref[...] = mod_coded
    cgrad_ref[...] = cond_back[0:1] * cond_sigmoid * (1.0 + cond * (1.0 - cond_sigmoid))

    flat2[o_end : flat2.shape[0], :] = jnp.zeros((flat2.shape[0] - o_end, LANES), F32)
    kept = keep_ref.shape[0]

    def own(slot, carry):
        owner = slot_owner(device, slot, out_bits, side)
        keep_ref[slot] = flat2[pl.ds(owner * rows_second, out_rows), :]
        return carry

    lax.fori_loop(0, kept, own, 0)
    for index, ref in enumerate(message_refs):

        def body(slot, carry, index=index, ref=ref):
            if core_masks[1:]:
                owner = slot_owner(device ^ core_masks[index + 1], slot, out_bits, side)
            else:
                owner = slot_owner(device, slot + (index + 1) * kept, out_bits, side)
            piece = flat2[pl.ds(owner * rows_second, out_rows), :]
            ref[pl.ds(pl.multiple_of(slot * out_rows, 16), out_rows), :] = encode(piece)
            return carry

        lax.fori_loop(0, kept, body, 0)
        ref[kept * out_rows : ref.shape[0], :] = mod_coded


def stage_kernel(out_rows, received, keep_ref, mod_ref, *refs):
    in_refs, out_refs = refs[:received], refs[received:]
    new_mod, new_keep = out_refs[:2]
    messages = out_refs[2:]
    kept = new_keep.shape[0]
    slots = keep_ref.shape[0]

    def total(slot):
        value = keep_ref[slot]
        for ref in in_refs:
            value = value + decode(ref[pl.ds(pl.multiple_of(slot * out_rows, 16), out_rows), :])
        return value

    def own(slot, carry):
        new_keep[slot] = total(slot)
        return carry

    lax.fori_loop(0, kept, own, 0)
    for index, ref in enumerate(messages):

        def body(slot, carry, index=index, ref=ref):
            value = total(slot + (index + 1) * kept)
            ref[pl.ds(pl.multiple_of(slot * out_rows, 16), out_rows), :] = encode(value)
            return carry

        lax.fori_loop(0, kept, body, 0)
    own_rows = mod_ref.shape[0]
    for target, start in [(new_mod, 0)] + [(ref, kept * out_rows) for ref in messages]:
        target[start : start + own_rows, :] = mod_ref[...]
        for index, ref in enumerate(in_refs):
            begin = start + (index + 1) * own_rows
            target[begin : begin + own_rows, :] = ref[slots * out_rows : ref.shape[0], :]


def last_kernel(rows_first, rows_second, D, mod_rows, info, keep_ref, mod_ref, *refs):
    *in_refs, second_ref, first_ref, gathered_ref, flat = refs
    device = info[0]
    out_rows = keep_ref.shape[1]
    value = keep_ref[0]
    for ref in in_refs:
        value = value + decode(ref[0:out_rows, :])
    second_ref[...] = value[:rows_second]

    coded_rows = wide_rows(mod_rows)
    slots = mod_ref.shape[0] // coded_rows
    for index, ref in enumerate([mod_ref, *in_refs]):
        start = 0 if index == 0 else out_rows

        def body(slot, carry, index=index, ref=ref, start=start):
            rows = pl.ds(pl.multiple_of(start + slot * coded_rows, 16), coded_rows)
            gathered_ref[index * slots + slot] = decode_wide(ref[rows, :], mod_rows)
            return carry

        lax.fori_loop(0, slots, body, 0)
    fr = D // LANES
    wide = 6 * fr
    images = gathered_ref.shape[0]
    first = (device * rows_first) // wide
    shift = device * rows_first - first * wide
    take = flat.shape[0] // wide
    picked = jnp.zeros((images, take), F32)
    for i in range(fr):
        rows = lax.broadcasted_iota(jnp.int32, (LANES, take), 0) + i * LANES
        chosen = lax.broadcasted_iota(jnp.int32, (LANES, take), 1) + first
        onehot = jnp.where(rows == chosen, 1.0, 0.0).astype(BF16)
        picked = picked + dot_nn(gathered_ref[:, wide + i, :].astype(BF16), onehot)
    picked = picked.astype(BF16)
    row_ids = lax.broadcasted_iota(jnp.int32, (take, LANES), 0) + first
    for j in range(wide):
        grads = gathered_ref[:, j, :]
        product = dot_tn(picked, grads.astype(BF16))
        total = jnp.sum(grads, axis=0, keepdims=True)
        flat[pl.ds(j, take, stride=wide), :] = jnp.where(row_ids == D, total, product)
    first_ref[...] = flat[pl.ds(shift, rows_first), :]


def vmem():
    return pl.BlockSpec(memory_space=pltpu.VMEM)


def on_device(mesh, block_input, conditioning, cotangent, image_counts, first_params, second_params):
    count = mesh.shape["fsdp"]
    images, tokens, D = block_input.shape
    core, links = axis_bits(mesh)
    device = lax.axis_index("fsdp").astype(jnp.int32)
    info = jnp.stack([device, image_counts[0]])
    rows_first = first_params.shape[0] // LANES
    rows_second = second_params.shape[0] // LANES
    pad_first, pad_second = up_to(rows_first, 16), up_to(rows_second, 16)

    def rows_of(vector, rows, padded):
        return jnp.pad(vector.reshape(rows, LANES), ((0, padded - rows), (0, 0)))

    shard = jnp.concatenate(
        [
            rows_of(second_params, rows_second, pad_second),
            rows_of(first_params, rows_first, pad_first),
        ]
    )
    stages = stages_of(core, links)
    segments = ((0, rows_second, True, 0), (pad_second, rows_first, False, 0))
    buffer = shard[None]
    held = []
    bits = ((), ())
    for index, stage in enumerate(stages):
        masks = pair_masks(stage)
        pieces = [buffer] + [swap(buffer, mask, count, core) for mask in masks[1:]]
        if index < len(stages) - 1:
            buffer = jnp.concatenate(pieces, axis=0)
            bits = tuple(bits[k] + tuple(stage[k]) for k in range(2))
        else:
            held = list(zip(pieces, masks))
    gathered, gather_parts = [], []
    for core_mask in masks_of(core):
        for piece, mask in held:
            moved = swap(piece, (core_mask, core_mask), count, core) if core_mask else piece
            gathered.append(moved)
            gather_parts.append((bits, mask, core_mask, segments))

    out_rows = up_to(rows_second + 1, 16)
    mod_rows = up_to(7 * D // LANES, 8)
    coded_rows = wide_rows(mod_rows)
    out_stages = [(core, core)] if core else []
    out_stages = out_stages + stages[::-1]
    out_bits = tuple(
        tuple(bit for stage in stages for bit in stage[k]) for k in range(2)
    )

    def out_shapes(slots, mods, stage):
        ways = len(pair_masks(stage))
        kept = slots // ways
        message = sds((kept * out_rows + mods * coded_rows, LANES), jnp.int16)
        return [
            sds((mods * coded_rows, LANES), jnp.int16),
            sds((kept, out_rows, LANES), F32),
        ], [message] * (ways - 1)

    sds = jax.ShapeDtypeStruct
    (mod_shape, keep_shape), message_shapes = out_shapes(count, 1, out_stages[0])
    n_chunks = MLP // CHUNK
    plan = (
        len(gathered),
        gather_parts,
        rows_first,
        rows_second,
        pad_second,
        out_bits,
        out_rows,
        masks_of(core),
        D,
    )
    results = pl.pallas_call(
        functools.partial(block_kernel, plan),
        out_shape=[
            sds((tokens, D), F32),
            sds((tokens, D), F32),
            sds((1, D), F32),
            mod_shape,
            keep_shape,
            *message_shapes,
        ],
        in_specs=[pl.BlockSpec(memory_space=pltpu.SMEM)] + [vmem()] * (3 + len(gathered)),
        out_specs=[vmem()] * (5 + len(message_shapes)),
        scratch_shapes=[
            pltpu.VMEM((count * rows_first, LANES), F32),
            pltpu.VMEM((count * rows_second + 16, LANES), F32),
            pltpu.VMEM((6 * D // LANES, D, LANES), BF16),
            pltpu.VMEM((D, 3 * D), BF16),
            pltpu.VMEM((D, D), BF16),
            pltpu.VMEM((n_chunks, D, CHUNK), BF16),
            pltpu.VMEM((n_chunks, CHUNK, D), BF16),
            pltpu.VMEM((8, 6 * D), F32),
            pltpu.VMEM((3 * D // LANES, tokens, LANES), BF16),
            pltpu.VMEM((HEADS, tokens, tokens), F32),
            pltpu.VMEM((tokens, D), BF16),
            pltpu.VMEM((n_chunks, tokens, CHUNK), BF16),
            pltpu.VMEM((n_chunks, tokens, CHUNK), F32),
            pltpu.VMEM((tokens, 3 * D), BF16),
            pltpu.VMEM((mod_rows, LANES), F32),
        ],
        compiler_params=pltpu.CompilerParams(vmem_limit_bytes=60 * 1024 * 1024),
        cost_estimate=pl.CostEstimate(
            flops=3 * 2 * tokens * D * 12 * D, bytes_accessed=16 << 20, transcendentals=1 << 20
        ),
        name="block",
    )(
        info,
        block_input.reshape(tokens, D),
        conditioning,
        cotangent.reshape(tokens, D),
        *gathered,
    )
    block_output, input_grad, cond_grad, mods, keep, *messages = results

    gathered_mods = 1
    for index, stage in enumerate(out_stages):
        masks = pair_masks(stage)[1:]
        received = [
            swap(message, mask, count, core)
            for message, mask in zip(messages, masks)
        ]
        gathered_mods *= len(masks) + 1
        if index == len(out_stages) - 1:
            break
        (mod_shape, keep_shape), message_shapes = out_shapes(
            keep.shape[0], gathered_mods, out_stages[index + 1]
        )
        mods, keep, *messages = pl.pallas_call(
            functools.partial(stage_kernel, out_rows, len(received)),
            out_shape=[mod_shape, keep_shape, *message_shapes],
            in_specs=[vmem()] * (2 + len(received)),
            out_specs=[vmem()] * (2 + len(message_shapes)),
            compiler_params=pltpu.CompilerParams(vmem_limit_bytes=60 * 1024 * 1024),
            name=f"stage{index}",
        )(keep, mods, *received)
    take = up_to((rows_first + 6 * D // LANES - 1) // (6 * D // LANES) + 1, 8)
    second_grad, first_grad = pl.pallas_call(
        functools.partial(last_kernel, rows_first, rows_second, D, mod_rows),
        out_shape=[sds((rows_second, LANES), F32), sds((rows_first, LANES), F32)],
        in_specs=[pl.BlockSpec(memory_space=pltpu.SMEM)] + [vmem()] * (2 + len(received)),
        out_specs=[vmem()] * 2,
        scratch_shapes=[
            pltpu.VMEM((count, mod_rows, LANES), F32),
            pltpu.VMEM((take * 6 * D // LANES, LANES), F32),
        ],
        name="last",
    )(info, keep, mods, *received)
    return (
        block_output.reshape(block_input.shape),
        input_grad.reshape(block_input.shape),
        cond_grad,
        first_grad.reshape(-1),
        second_grad.reshape(-1),
    )


def solution(mesh):
    return jax.shard_map(
        functools.partial(on_device, mesh),
        mesh=mesh,
        in_specs=(
            P("fsdp", None, None),
            P("fsdp", None),
            P("fsdp", None, None),
            P("fsdp"),
            P("fsdp"),
            P("fsdp"),
        ),
        out_specs=(
            P("fsdp", None, None),
            P("fsdp", None, None),
            P("fsdp", None),
            P("fsdp"),
            P("fsdp"),
        ),
        check_vma=False,
    )
```

```python
import functools
import math

import jax
import jax.numpy as jnp
from jax import lax
from jax.experimental import pallas as pl
from jax.experimental.pallas import tpu as pltpu
from jax.sharding import PartitionSpec as P

HEADS = 6
HEAD_DIM = 64
MLP = 1536
LANES = 128
CHUNK = 256

EPS = 1e-06
GELU_K = 0.7978845608028654
GELU_C = 0.044715


F32 = jnp.float32
BF16 = jnp.bfloat16


def axis_bits(mesh):
    devices = list(mesh.devices.flat)
    count = len(devices)

    def place(device):
        coords = getattr(device, "coords", None)
        if coords is None:
            return None
        return (*coords, getattr(device, "core_on_chip", 0))

    groups = {}
    bit = 1
    while bit < count:
        start, end = place(devices[0]), place(devices[bit])
        if start is None:
            key = 3 if bit == 1 else bit + 100
        else:
            key = next(axis for axis in range(4) if start[axis] != end[axis])
        groups.setdefault(key, []).append(bit)
        bit *= 2
    core = groups.pop(3, [])
    links = sorted(groups.values(), key=lambda bits: (-len(bits), bits))
    return core, links


def stages_of(core, links):
    other = links[:1] + links[1:][::-1]
    if not core or [len(bits) for bits in other] != [len(bits) for bits in links]:
        other = links
    return list(zip(links, other))


def masks_of(bits):
    masks = [0]
    for bit in bits:
        masks = masks + [mask | bit for mask in masks]
    return masks


def pair_masks(stage):
    return list(zip(masks_of(stage[0]), masks_of(stage[1])))


def swap(values, masks, count, core):
    side = sum(core)
    pairs = [(index, index ^ masks[1 if index & side else 0]) for index in range(count)]
    return lax.ppermute(values, "fsdp", pairs)


def up_to(value, multiple):
    return -(-value // multiple) * multiple


def dot_nn(left, right):
    return lax.dot_general(left, right, (((1,), (0,)), ((), ())), preferred_element_type=F32)


def dot_nt(left, right):
    return lax.dot_general(left, right, (((1,), (1,)), ((), ())), preferred_element_type=F32)


def dot_tn(left, right):
    return lax.dot_general(left, right, (((0,), (0,)), ((), ())), preferred_element_type=F32)


def slot_owner(device, slot, bit_pair, side):
    offsets = []
    for bits in bit_pair:
        offset = 0
        for position, bit in enumerate(bits):
            offset = offset + ((slot >> position) & 1) * bit
        offsets.append(offset)
    if bit_pair[0] == bit_pair[1]:
        return device ^ offsets[0]
    return device ^ jnp.where((device & side) > 0, offsets[1], offsets[0])


TOP = 32000.0


def exponent_of(values):
    top = jnp.max(jnp.abs(values), axis=0, keepdims=True)
    return jnp.ceil(jnp.log2(jnp.maximum(top, 1e-30) * (1.0 / TOP)))


def nearest(values):
    return jnp.floor(values + 0.5)


def encode(values):
    rows = values.shape[0]
    exponent = exponent_of(values)
    coded = nearest(values * jnp.exp2(-exponent))
    last = lax.broadcasted_iota(jnp.int32, values.shape, 0) == rows - 1
    return jnp.where(last, exponent, coded).astype(jnp.int32).astype(jnp.int16)


def decode(coded):
    wide = coded.astype(jnp.int32).astype(F32)
    return wide * jnp.exp2(wide[coded.shape[0] - 1 :])


def encode_wide(values, used):
    exponent = exponent_of(values)
    scaled = values * jnp.exp2(-exponent)
    high = nearest(scaled)
    low = nearest((scaled - high) * TOP)
    spare = lax.broadcasted_iota(jnp.int32, values.shape, 0) >= used
    coded = jnp.concatenate([jnp.where(spare, exponent, high), low])
    return coded.astype(jnp.int32).astype(jnp.int16)


def decode_wide(coded):
    rows = coded.shape[0] // 2
    wide = coded.astype(jnp.int32).astype(F32)
    value = wide[:rows] + wide[rows:] * (1.0 / TOP)
    return value * jnp.exp2(wide[rows - 1 : rows])


def layer_norm(values):
    centered = values - jnp.mean(values, axis=-1, keepdims=True)
    inverse = lax.rsqrt(jnp.mean(centered * centered, axis=-1, keepdims=True) + EPS)
    return centered * inverse, inverse


def norm_back(upstream, normed, inverse):
    return inverse * (
        upstream
        - jnp.mean(upstream, axis=-1, keepdims=True)
        - normed * jnp.mean(upstream * normed, axis=-1, keepdims=True)
    )


def block_kernel(
    plan,
    info,
    x_ref,
    cond_ref,
    cot_ref,
    *refs,
):
    (n_in, gather_parts, rows_first, rows_second, pad_second, out_parts, core_masks, D) = plan
    side = core_masks[-1]
    part_refs = refs[:n_in]
    out_ref, xgrad_ref, cgrad_ref, mod_out_ref = refs[n_in : n_in + 4]
    keep_refs = refs[n_in + 4 : n_in + 4 + len(out_parts)]
    message_refs = refs[n_in + 4 + len(out_parts) : -15]
    (
        flat1,
        flat2,
        wada,
        wqkv,
        wproj,
        wf1,
        wf2,
        mod_ref,
        qkv,
        prob,
        mixed,
        act,
        slope,
        dqkv,
        mod_rows_ref,
    ) = refs[-15:]
    device = info[0]
    valid = jnp.where(info[1] > 0, 1.0, 0.0).astype(F32)
    fr = D // LANES
    n_chunks = MLP // CHUNK
    cr = CHUNK // LANES
    mr = MLP // LANES

    for ref, (bits, mask, shift, core_mask, segments) in zip(part_refs, gather_parts):

        def body(
            slot,
            carry,
            ref=ref,
            bits=bits,
            mask=mask,
            shift=shift,
            core_mask=core_mask,
            segments=segments,
        ):
            base = device ^ core_mask
            owner = slot_owner(base, slot + shift, bits, side)
            if mask[0] == mask[1]:
                owner = owner ^ mask[0]
            else:
                owner = owner ^ jnp.where((base & side) > 0, mask[1], mask[0])
            for start, size, second, target in segments:
                piece = ref[slot, start : start + size, :].astype(F32)
                if second:
                    flat2[pl.ds(owner * rows_second + target, size), :] = piece
                else:
                    flat1[pl.ds(owner * rows_first + target, size), :] = piece
            return carry

        lax.fori_loop(0, ref.shape[0], body, 0)

    cond = cond_ref[...]
    cond_sigmoid = jax.nn.sigmoid(cond)
    cond_act = cond * cond_sigmoid
    cond_low = jnp.broadcast_to(cond_act.astype(BF16), (16, D))
    for j in range(6 * fr):
        w = flat1[pl.ds(j, D, stride=6 * fr), :].astype(BF16)
        wada[j] = w
        bias = flat1[pl.ds(6 * fr * D + j, 1), :]
        mod_ref[0:1, j * LANES : (j + 1) * LANES] = dot_nn(cond_low, w)[0:1] + bias

    def mod_piece(index):
        return mod_ref[0:1, index * D : (index + 1) * D]

    o_bqv = 3 * fr * D
    o_proj = o_bqv + 2 * fr
    o_bproj = o_proj + fr * D
    o_fc1 = o_bproj + fr
    o_b1 = o_fc1 + mr * D
    o_fc2 = o_b1 + mr
    o_b2 = o_fc2 + fr * MLP
    o_end = o_b2 + fr
    for j in range(3 * fr):
        wqkv[:, j * LANES : (j + 1) * LANES] = flat2[pl.ds(j, D, stride=3 * fr), :].astype(BF16)
    for j in range(fr):
        wproj[:, j * LANES : (j + 1) * LANES] = flat2[pl.ds(o_proj + j, D, stride=fr), :].astype(
            BF16
        )
    for c in range(n_chunks):
        for j in range(cr):
            wf1[c, :, j * LANES : (j + 1) * LANES] = flat2[
                pl.ds(o_fc1 + c * cr + j, D, stride=mr), :
            ].astype(BF16)
        for j in range(fr):
            wf2[c, :, j * LANES : (j + 1) * LANES] = flat2[
                pl.ds(o_fc2 + c * CHUNK * fr + j, CHUNK, stride=fr), :
            ].astype(BF16)

    def bias_row(start, rows):
        return jnp.concatenate([flat2[pl.ds(start + i, 1), :] for i in range(rows)], axis=1)

    block_input = x_ref[...]
    normed_one, inverse_one = layer_norm(block_input)
    moved_one = (normed_one * (1.0 + mod_piece(1)) + mod_piece(0)).astype(BF16)
    projected = dot_nn(moved_one, wqkv[...])
    bias_qv = bias_row(o_bqv, 2 * fr)
    for j in range(fr):
        cols = slice(j * LANES, (j + 1) * LANES)
        qkv[j] = (projected[:, cols] + bias_qv[:, cols]).astype(BF16)
        qkv[fr + j] = projected[:, D + j * LANES : D + (j + 1) * LANES].astype(BF16)
        qkv[2 * fr + j] = (
            projected[:, 2 * D + j * LANES : 2 * D + (j + 1) * LANES]
            + bias_qv[:, D + j * LANES : D + (j + 1) * LANES]
        ).astype(BF16)
    scale_factor = 1.0 / math.sqrt(HEAD_DIM)
    low_lane = lax.broadcasted_iota(jnp.int32, (1, LANES), 1) < HEAD_DIM
    lane_masks = [
        jnp.where(low_lane, 1.0, 0.0).astype(BF16),
        jnp.where(low_lane, 0.0, 1.0).astype(BF16),
    ]
    for p in range(fr):
        q, k, v = qkv[p], qkv[fr + p], qkv[2 * fr + p]
        outs = []
        for h in range(2):
            scores = dot_nt(q * lane_masks[h], k) * scale_factor
            raised = jnp.exp(scores - jnp.max(scores, axis=1, keepdims=True))
            probability = raised * (1.0 / jnp.sum(raised, axis=1, keepdims=True))
            prob[2 * p + h] = probability
            outs.append(dot_nn(probability.astype(BF16), v))
        mixed[:, p * LANES : (p + 1) * LANES] = jnp.where(low_lane, outs[0], outs[1]).astype(BF16)
    attn_out = dot_nn(mixed[...], wproj[...]) + bias_row(o_bproj, fr)
    after_attn = block_input + mod_piece(2) * attn_out
    normed_two, inverse_two = layer_norm(after_attn)
    moved_two = (normed_two * (1.0 + mod_piece(4)) + mod_piece(3)).astype(BF16)

    mlp_out = jnp.zeros_like(after_attn) + bias_row(o_b2, fr)
    for c in range(n_chunks):
        hidden = dot_nn(moved_two, wf1[c]) + bias_row(o_b1 + c * cr, cr)
        square = hidden * hidden
        tangent = jnp.tanh(GELU_K * (hidden + GELU_C * square * hidden))
        half = 0.5 * (1.0 + tangent)
        low = (hidden * half).astype(BF16)
        act[c] = low
        slope[c] = half + 0.5 * hidden * (1.0 - tangent * tangent) * (
            GELU_K + (3.0 * GELU_C * GELU_K) * square
        )
        mlp_out = mlp_out + dot_nn(low, wf2[c])
    gate_mlp = mod_piece(5)
    out_ref[...] = valid * (after_attn + gate_mlp * mlp_out)

    masked = valid * cot_ref[...]
    gate_grad_mlp = jnp.sum(masked * mlp_out, axis=0, keepdims=True)
    out_grad = masked * gate_mlp
    out_grad_low = out_grad.astype(BF16)

    def put_row(start, row):
        for i in range(row.shape[1] // LANES):
            flat2[pl.ds(start + i, 1), :] = row[:, i * LANES : (i + 1) * LANES]

    put_row(o_b2, jnp.sum(out_grad, axis=0, keepdims=True))
    moved_grad = jnp.zeros_like(after_attn)
    for c in range(n_chunks):
        pre_grad = dot_nt(out_grad_low, wf2[c]) * slope[c]
        put_row(o_b1 + c * cr, jnp.sum(pre_grad, axis=0, keepdims=True))
        pre_low = pre_grad.astype(BF16)
        grad2 = dot_tn(act[c], out_grad_low)
        for j in range(fr):
            flat2[pl.ds(o_fc2 + c * CHUNK * fr + j, CHUNK, stride=fr), :] = grad2[
                :, j * LANES : (j + 1) * LANES
            ]
        grad1 = dot_tn(moved_two, pre_low)
        for j in range(cr):
            flat2[pl.ds(o_fc1 + c * cr + j, D, stride=mr), :] = grad1[
                :, j * LANES : (j + 1) * LANES
            ]
        moved_grad = moved_grad + dot_nt(pre_low, wf1[c])
    shift_grad_mlp = jnp.sum(moved_grad, axis=0, keepdims=True)
    scale_grad_mlp = jnp.sum(moved_grad * normed_two, axis=0, keepdims=True)
    grad_after = masked + norm_back(moved_grad * (1.0 + mod_piece(4)), normed_two, inverse_two)

    gate_grad_attn = jnp.sum(grad_after * attn_out, axis=0, keepdims=True)
    proj_grad = grad_after * mod_piece(2)
    proj_low = proj_grad.astype(BF16)
    grad_proj = dot_tn(mixed[...], proj_low)
    for j in range(fr):
        flat2[pl.ds(o_proj + j, D, stride=fr), :] = grad_proj[:, j * LANES : (j + 1) * LANES]
    put_row(o_bproj, jnp.sum(proj_grad, axis=0, keepdims=True))
    mixed_grad = dot_nt(proj_low, wproj[...]).astype(BF16)
    for p in range(fr):
        q, k, v = qkv[p], qkv[fr + p], qkv[2 * fr + p]
        cols = slice(p * LANES, (p + 1) * LANES)
        pair_grad = mixed_grad[:, cols]
        product = pair_grad.astype(F32) * mixed[:, cols].astype(F32)
        pieces = []
        for h in range(2):
            probability = prob[2 * p + h]
            value_grad = dot_tn(probability.astype(BF16), pair_grad)
            prob_grad = dot_nt(pair_grad * lane_masks[h], v)
            own = jnp.where(low_lane, product, 0.0) if h == 0 else jnp.where(low_lane, 0.0, product)
            row_dot = jnp.sum(own, axis=1, keepdims=True)
            score_grad = (probability * (prob_grad - row_dot) * scale_factor).astype(BF16)
            pieces.append((dot_nn(score_grad, k), dot_tn(score_grad, q), value_grad))
        for index in range(3):
            grad = jnp.where(low_lane, pieces[0][index], pieces[1][index])
            if index != 1:
                put_row(
                    o_bqv + (0 if index == 0 else fr) + p, jnp.sum(grad, axis=0, keepdims=True)
                )
            dqkv[:, index * D + p * LANES : index * D + (p + 1) * LANES] = grad.astype(BF16)
    grad_qkv = dot_tn(moved_one, dqkv[...])
    for j in range(3 * fr):
        flat2[pl.ds(j, D, stride=3 * fr), :] = grad_qkv[:, j * LANES : (j + 1) * LANES]
    moved_grad_one = dot_nt(dqkv[...], wqkv[...])
    shift_grad_attn = jnp.sum(moved_grad_one, axis=0, keepdims=True)
    scale_grad_attn = jnp.sum(moved_grad_one * normed_one, axis=0, keepdims=True)
    xgrad_ref[...] = grad_after + norm_back(
        moved_grad_one * (1.0 + mod_piece(1)), normed_one, inverse_one
    )

    mod_rows = [
        shift_grad_attn,
        scale_grad_attn,
        gate_grad_attn,
        shift_grad_mlp,
        scale_grad_mlp,
        gate_grad_mlp,
    ]
    cond_back = jnp.zeros((16, D), F32)
    mod_rows_ref[...] = jnp.zeros_like(mod_rows_ref)
    for index, row in enumerate(mod_rows):
        for i in range(fr):
            j = index * fr + i
            piece = row[:, i * LANES : (i + 1) * LANES]
            mod_rows_ref[j : j + 1, :] = piece
            low = jnp.broadcast_to(piece.astype(BF16), (16, LANES))
            cond_back = cond_back + dot_nt(low, wada[j])
    for i in range(fr):
        j = 6 * fr + i
        mod_rows_ref[j : j + 1, :] = cond_act.astype(BF16).astype(F32)[
            :, i * LANES : (i + 1) * LANES
        ]
    mod_coded = encode_wide(mod_rows_ref[...], 7 * fr)
    mod_out_ref[...] = mod_coded
    cgrad_ref[...] = cond_back[0:1] * cond_sigmoid * (1.0 + cond * (1.0 - cond_sigmoid))

    flat2[o_end : flat2.shape[0], :] = jnp.zeros((flat2.shape[0] - o_end, LANES), F32)
    base = 0
    for keep_ref, (bits, start, rows) in zip(keep_refs, out_parts):
        kept = keep_ref.shape[0]

        def own(slot, carry, keep_ref=keep_ref, bits=bits, start=start, rows=rows):
            owner = slot_owner(device, slot, bits, side)
            keep_ref[slot] = flat2[pl.ds(owner * rows_second + start, rows), :]
            return carry

        lax.fori_loop(0, kept, own, 0)
        for mask, ref in zip(core_masks[1:], message_refs):

            def body(
                slot, carry, mask=mask, ref=ref, bits=bits, start=start, rows=rows, base=base
            ):
                owner = slot_owner(device ^ mask, slot, bits, side)
                piece = flat2[pl.ds(owner * rows_second + start, rows), :]
                ref[pl.ds(pl.multiple_of(base + slot * rows, 16), rows), :] = encode(piece)
                return carry

            lax.fori_loop(0, kept, body, 0)
        base += kept * rows
    for ref in message_refs:
        ref[base : ref.shape[0], :] = mod_coded


def stage_kernel(rows, received, base, with_mods, *refs):
    if with_mods:
        mod_ref, *refs = refs
    keep_ref, *refs = refs
    in_refs, out_refs = refs[:received], refs[received:]
    if with_mods:
        new_mod, *out_refs = out_refs
    new_keep, *messages = out_refs
    kept = new_keep.shape[0]

    def total(slot):
        value = keep_ref[slot]
        for ref in in_refs:
            value = value + decode(ref[pl.ds(pl.multiple_of(base + slot * rows, 16), rows), :])
        return value

    for index, ref in enumerate(messages):

        def body(slot, carry, index=index, ref=ref):
            value = total(slot + (index + 1) * kept)
            ref[pl.ds(pl.multiple_of(slot * rows, 16), rows), :] = encode(value)
            return carry

        lax.fori_loop(0, kept, body, 0)

    def own(slot, carry):
        new_keep[slot] = total(slot)
        return carry

    lax.fori_loop(0, kept, own, 0)
    if with_mods:
        own_rows = mod_ref.shape[0]
        for target, start in [(new_mod, 0)] + [(ref, kept * rows) for ref in messages]:
            target[start : start + own_rows, :] = mod_ref[...]
            for index, ref in enumerate(in_refs):
                begin = start + (index + 1) * own_rows
                target[begin : begin + own_rows, :] = ref[ref.shape[0] - own_rows :, :]


def last_kernel(rows_first, data_rows, received, D, coded_rows, info, *refs):
    keep_refs, mod_ref, refs = refs[:2], refs[2], refs[3:]
    in_refs = [refs[: received[0]], refs[received[0] : sum(received)]]
    second_ref, first_ref, gathered_ref, flat = refs[sum(received) :]
    device = info[0]
    start = 0
    for keep_ref, ins, data in zip(keep_refs, in_refs, data_rows):
        value = keep_ref[0]
        for ref in ins:
            value = value + decode(ref[0 : value.shape[0], :])
        second_ref[start : start + data, :] = value[:data]
        start += data

    slots = mod_ref.shape[0] // coded_rows
    for index, ref in enumerate([mod_ref, *in_refs[1]]):
        base = 0 if index == 0 else keep_refs[1].shape[1]

        def body(slot, carry, index=index, ref=ref, base=base):
            rows = pl.ds(pl.multiple_of(base + slot * coded_rows, 16), coded_rows)
            gathered_ref[index * slots + slot] = decode_wide(ref[rows, :])
            return carry

        lax.fori_loop(0, slots, body, 0)
    fr = D // LANES
    wide = 6 * fr
    images = gathered_ref.shape[0]
    first = (device * rows_first) // wide
    shift = device * rows_first - first * wide
    take = flat.shape[0] // wide
    picked = jnp.zeros((images, take), F32)
    for i in range(fr):
        rows = lax.broadcasted_iota(jnp.int32, (LANES, take), 0) + i * LANES
        chosen = lax.broadcasted_iota(jnp.int32, (LANES, take), 1) + first
        onehot = jnp.where(rows == chosen, 1.0, 0.0).astype(BF16)
        picked = picked + dot_nn(gathered_ref[:, wide + i, :].astype(BF16), onehot)
    picked = picked.astype(BF16)
    row_ids = lax.broadcasted_iota(jnp.int32, (take, LANES), 0) + first
    for j in range(wide):
        grads = gathered_ref[:, j, :]
        product = dot_tn(picked, grads.astype(BF16))
        total = jnp.sum(grads, axis=0, keepdims=True)
        flat[pl.ds(j, take, stride=wide), :] = jnp.where(row_ids == D, total, product)
    first_ref[...] = flat[pl.ds(shift, rows_first), :]


def vmem():
    return pl.BlockSpec(memory_space=pltpu.VMEM)


def on_device(mesh, block_input, conditioning, cotangent, image_counts, first_params, second_params):
    count = mesh.shape["fsdp"]
    images, tokens, D = block_input.shape
    core, links = axis_bits(mesh)
    device = lax.axis_index("fsdp").astype(jnp.int32)
    info = jnp.stack([device, image_counts[0]])
    rows_first = first_params.shape[0] // LANES
    rows_second = second_params.shape[0] // LANES
    pad_first, pad_second = up_to(rows_first, 16), up_to(rows_second, 16)

    def rows_of(vector, rows, padded):
        return jnp.pad(vector.reshape(rows, LANES), ((0, padded - rows), (0, 0)))

    shard = jnp.concatenate(
        [
            rows_of(second_params, rows_second, pad_second),
            rows_of(first_params, rows_first, pad_first),
        ]
    )
    stages = stages_of(core, links)
    turned = stages[1:] + stages[:1]
    tiles = shard.shape[0] // 16
    middle = 16 * (tiles - max(1, round(0.28 * tiles)))
    gathered, gather_parts = [], []
    parts = []
    for start, end, order in ((0, middle, stages), (middle, 16 * tiles, turned)):
        segments = []
        low, high = start, min(end, rows_second)
        if low < high:
            segments.append((0, high - low, True, low))
        low, high = max(start, pad_second), min(end, pad_second + rows_first)
        if low < high:
            segments.append((low - start, high - low, False, low - pad_second))
        parts.append([shard[None, start:end], ((), ()), order, tuple(segments)])
    core_masks = masks_of(core)
    for index in range(len(stages)):
        for part in parts:
            buffer, bits, order, segments = part
            masks = pair_masks(order[index])
            pieces = [buffer] + [swap(buffer, mask, count, core) for mask in masks[1:]]
            joined = tuple(bits[k] + tuple(order[index][k]) for k in range(2))
            if index < len(stages) - 1:
                part[:2] = jnp.concatenate(pieces, axis=0), joined
                continue
            ways = [(buffer, bits, masks[0])]
            if len(masks) == 2:
                ways.append((pieces[1], bits, masks[1]))
            else:
                ways.append((jnp.concatenate(pieces[1:], axis=0), joined, None))
            for core_mask in core_masks:
                for piece, piece_bits, mask in ways:
                    moved = piece
                    if core_mask:
                        moved = swap(piece, (core_mask, core_mask), count, core)
                    gathered.append(moved)
                    shift = 0 if mask else buffer.shape[0]
                    gather_parts.append(
                        (piece_bits, mask or (0, 0), shift, core_mask, segments)
                    )

    tiles = up_to(rows_second + 2, 16) // 16
    part_rows = [16 * (tiles - max(1, round(0.28 * tiles)))]
    data_rows = [part_rows[0] - 1, rows_second - part_rows[0] + 1]
    part_rows.append(up_to(data_rows[1] + 1, 16))
    out_orders = [stages[::-1], turned[::-1]]
    out_parts = []
    for i in range(2):
        bits = tuple(
            tuple(bit for stage in out_orders[i][::-1] for bit in stage[k]) for k in range(2)
        )
        out_parts.append((bits, sum(data_rows[:i]), part_rows[i]))
    mod_rows = up_to(7 * D // LANES + 1, 8)
    coded_rows = 2 * mod_rows
    sds = jax.ShapeDtypeStruct
    slots = count // len(core_masks)
    message_shape = sds((slots * sum(part_rows) + coded_rows, LANES), jnp.int16)
    n_chunks = MLP // CHUNK
    plan = (
        len(gathered),
        gather_parts,
        rows_first,
        rows_second,
        pad_second,
        tuple(out_parts),
        core_masks,
        D,
    )
    results = pl.pallas_call(
        functools.partial(block_kernel, plan),
        out_shape=[
            sds((tokens, D), F32),
            sds((tokens, D), F32),
            sds((1, D), F32),
            sds((coded_rows, LANES), jnp.int16),
            *[sds((slots, rows, LANES), F32) for rows in part_rows],
            *[message_shape] * (len(core_masks) - 1),
        ],
        in_specs=[pl.BlockSpec(memory_space=pltpu.SMEM)] + [vmem()] * (3 + len(gathered)),
        out_specs=[vmem()] * (5 + len(core_masks)),
        scratch_shapes=[
            pltpu.VMEM((count * rows_first, LANES), F32),
            pltpu.VMEM((count * rows_second + 16, LANES), F32),
            pltpu.VMEM((6 * D // LANES, D, LANES), BF16),
            pltpu.VMEM((D, 3 * D), BF16),
            pltpu.VMEM((D, D), BF16),
            pltpu.VMEM((n_chunks, D, CHUNK), BF16),
            pltpu.VMEM((n_chunks, CHUNK, D), BF16),
            pltpu.VMEM((8, 6 * D), F32),
            pltpu.VMEM((3 * D // LANES, tokens, LANES), BF16),
            pltpu.VMEM((HEADS, tokens, tokens), F32),
            pltpu.VMEM((tokens, D), BF16),
            pltpu.VMEM((n_chunks, tokens, CHUNK), BF16),
            pltpu.VMEM((n_chunks, tokens, CHUNK), F32),
            pltpu.VMEM((tokens, 3 * D), BF16),
            pltpu.VMEM((mod_rows, LANES), F32),
        ],
        compiler_params=pltpu.CompilerParams(vmem_limit_bytes=48 * 1024 * 1024),
        cost_estimate=pl.CostEstimate(
            flops=3 * 2 * tokens * D * 12 * D, bytes_accessed=16 << 20, transcendentals=1 << 20
        ),
        name="block",
    )(
        info,
        block_input.reshape(tokens, D),
        conditioning,
        cotangent.reshape(tokens, D),
        *gathered,
    )
    block_output, input_grad, cond_grad, mods = results[:4]
    keeps = list(results[4:6])
    messages = results[6:]

    arrived = [
        swap(message, (mask, mask), count, core)
        for message, mask in zip(messages, core_masks[1:])
    ]
    received = [arrived, arrived]
    bases = [0, slots * part_rows[0]]
    for index in range(len(stages)):
        for i in range(2):
            masks = pair_masks(out_orders[i][index])
            kept = keeps[i].shape[0] // len(masks)
            rows = part_rows[i]
            mod_in = [mods] if i else []
            mod_shapes = []
            if i:
                mod_shapes = [sds((mods.shape[0] * (len(received[i]) + 1), LANES), jnp.int16)]
            tail = mod_shapes[0].shape[0] if i else 0
            message = sds((kept * rows + tail, LANES), jnp.int16)
            outs = [*mod_shapes, sds((kept, rows, LANES), F32), *[message] * (len(masks) - 1)]
            results = pl.pallas_call(
                functools.partial(stage_kernel, rows, len(received[i]), bases[i], bool(i)),
                out_shape=outs,
                in_specs=[vmem()] * (len(mod_in) + 1 + len(received[i])),
                out_specs=[vmem()] * len(outs),
                compiler_params=pltpu.CompilerParams(vmem_limit_bytes=24 * 1024 * 1024),
                name=f"stage{index}part{i}",
            )(*mod_in, keeps[i], *received[i])
            if i:
                mods, *results = results
            keeps[i], *messages = results
            received[i] = [
                swap(message, mask, count, core) for message, mask in zip(messages, masks[1:])
            ]
            bases[i] = 0
    take = up_to((rows_first + 6 * D // LANES - 1) // (6 * D // LANES) + 1, 8)
    second_grad, first_grad = pl.pallas_call(
        functools.partial(
            last_kernel, rows_first, data_rows, [len(ins) for ins in received], D, coded_rows
        ),
        out_shape=[sds((rows_second, LANES), F32), sds((rows_first, LANES), F32)],
        in_specs=[pl.BlockSpec(memory_space=pltpu.SMEM)]
        + [vmem()] * (3 + len(received[0]) + len(received[1])),
        out_specs=[vmem()] * 2,
        scratch_shapes=[
            pltpu.VMEM((count, mod_rows, LANES), F32),
            pltpu.VMEM((take * 6 * D // LANES, LANES), F32),
        ],
        name="last",
    )(info, *keeps, mods, *received[0], *received[1])
    return (
        block_output.reshape(block_input.shape),
        input_grad.reshape(block_input.shape),
        cond_grad,
        first_grad.reshape(-1),
        second_grad.reshape(-1),
    )


def solution(mesh):
    return jax.shard_map(
        functools.partial(on_device, mesh),
        mesh=mesh,
        in_specs=(
            P("fsdp", None, None),
            P("fsdp", None),
            P("fsdp", None, None),
            P("fsdp"),
            P("fsdp"),
            P("fsdp"),
        ),
        out_specs=(
            P("fsdp", None, None),
            P("fsdp", None, None),
            P("fsdp", None),
            P("fsdp"),
            P("fsdp"),
        ),
        check_vma=False,
    )
```
